32 devices in a mesh: dp: 8 (over z, x), tensor: 4 (over y, core).
Axes of the slice: x: 2, y: 2, z: 4, core: 2. Of those that a mesh axis runs over, the one named last changes fastest.
Arguments:
- tokens: bfloat16 [8192, 1152], P('dp'), may hold values from -6 to 6
- condition: float32 [8, 1152], P('dp', 'tensor'), may hold values from -9 to 9, as said below
- ada_weight: bfloat16 [1152, 6912], P('tensor'), may hold values from -0.1875 to 0.1875
- ada_bias: float32 [6912], replicated, may hold values from -4 to 4
- query_weight: bfloat16 [1152, 1152], P(None, 'tensor'), may hold values from -0.1875 to 0.1875
- query_bias: float32 [1152], P('tensor'), may hold values from -4 to 4
- key_weight: bfloat16 [1152, 1152], P(None, 'tensor'), may hold values from -0.1875 to 0.1875
- value_weight: bfloat16 [1152, 1152], P(None, 'tensor'), may hold values from -0.1875 to 0.1875
- value_bias: float32 [1152], P('tensor'), may hold values from -4 to 4
- out_weight: bfloat16 [1152, 1152], P('tensor'), may hold values from -0.75 to 0.75
- out_bias: float32 [1152], replicated, may hold values from -4 to 4
- up_weight: bfloat16 [1152, 4608], P(None, 'tensor'), may hold values from -0.1875 to 0.1875
- up_bias: float32 [4608], P('tensor'), may hold values from -4 to 4
- down_weight: bfloat16 [4608, 1152], P('tensor'), may hold values from -0.09375 to 0.09375
- down_bias: float32 [1152], replicated, may hold values from -4 to 4
- clip_limit: float32 [16], P('tensor'), may hold values from 0.5 to 800, as said below
- cotangent: bfloat16 [8192, 1152], P('dp'), may hold values from -6 to 6
Outputs:
- block_out: bfloat16 [8192, 1152], P(('dp', 'tensor'))
- grad_tokens: bfloat16 [8192, 1152], P(('dp', 'tensor'))
- grad_condition: float32 [8, 1152], P('dp', 'tensor')
- grad_ada_weight: float32 [1152, 6912], P('tensor')
- grad_ada_bias: float32 [6912], replicated
- grad_query_weight: float32 [1152, 1152], P(None, 'tensor')
- grad_query_bias: float32 [1152], P('tensor')
- grad_key_weight: float32 [1152, 1152], P(None, 'tensor')
- grad_value_weight: float32 [1152, 1152], P(None, 'tensor')
- grad_value_bias: float32 [1152], P('tensor')
- grad_out_weight: float32 [1152, 1152], P('tensor')
- grad_out_bias: float32 [1152], replicated
- grad_up_weight: float32 [1152, 4608], P(None, 'tensor')
- grad_up_bias: float32 [4608], P('tensor')
- grad_down_weight: float32 [4608, 1152], P('tensor')
- grad_down_bias: float32 [1152], replicated
- head_max: float32 [16], P('tensor')
- clipped_query_weight: float32 [1152, 1152], P(None, 'tensor')
- clipped_query_bias: float32 [1152], P('tensor')
- clipped_key_weight: float32 [1152, 1152], P(None, 'tensor')
The draws below stay inside these ranges and needn't reach their ends.
Inputs may be any that keep to these rules, and one draw needn't show every extreme that they name: `condition`: the conditioning vectors are drawn on a scale that grows with the latent index (later latents are larger in scale, not element by element). `clip_limit`: 8 of the heads, which ones drawn from the seed, have a limit of 0.5 to 2; the others have a limit of 200 to 800.
All inputs are finite; a program needn't handle non-finite values.
Results may differ from the reference program's by a relative error of at most 0.018.
The reference program's roundings to bfloat16 on the way count: a program that leaves them out, or rounds other values in their place, can miss the bound.
Values may be sent and summed in bfloat16 or wider, within the bound.
No kernel may reach another device: no remote copies, remote signals or barrier semaphores. Data moves between devices by JAX's collectives and lax.ppermute only.
A program may use at most 192 MiB of HBM per device.

```python
import math
import jax
import jax.numpy as jnp
from jax import lax

D = 1152
H = 16
HD = 72
FF = 4608
SEQ = 1024
LATENTS = 8
TOKENS = 8192


def draw_condition(key, part):
    entries = jnp.clip(jax.random.normal(key, (LATENTS, D), jnp.float32), -5.0, 5.0)
    ramp = jnp.arange(LATENTS, dtype=jnp.float32) / max(LATENTS - 1, 1)
    return entries * (0.6 * jnp.exp(ramp * math.log(3.0)))[:, None]


def draw_clip_limit(key, part):
    order = jax.random.permutation(jax.random.fold_in(key, 11), H)
    lower = order < H // 2
    spread = jax.random.uniform(jax.random.fold_in(key, 12), (H,), jnp.float32, 0.0, 1.0)
    ratio = jnp.exp(spread * math.log(4.0))
    return jnp.where(lower, 0.5 * ratio, 200.0 * ratio).astype(jnp.float32)


def block_scale(stream_key, shape, shards, least, top_value):
    loudness = 1.0
    for axis_at, shards_of in shards:
        heights = jax.random.uniform(jax.random.fold_in(jax.random.fold_in(stream_key, 6), axis_at), (shards_of,), jnp.float32, least / len(shards), top_value / len(shards))
        loudness = loudness * jnp.repeat(jnp.exp(heights), shape[axis_at] // shards_of).reshape((-1,) + (1,) * (len(shape) - 1 - axis_at))
    return loudness


def scatter_about(stream_key, shape, deviation, most, cuts=(), held_as=jnp.bfloat16):
    values = deviation * jax.random.normal(stream_key, shape, jnp.float32)
    if cuts:
        values = values * block_scale(stream_key, shape, cuts, -0.22, 0.18)
    return jnp.clip(values, -most, most).astype(held_as)


def setup_inputs(seed: int = 0) -> dict:
    key_of = jax.random.split(jax.random.key(seed), 18)
    return {
        "tokens": scatter_about(key_of[0], (TOKENS, D), 1.0, 6.0, ((0, 8),)),
        "condition": draw_condition(jax.random.fold_in(key_of[17], 71), 0),
        "ada_weight": scatter_about(key_of[2], (D, 6 * D), D ** -0.5, 0.1875, ((0, 4),)),
        "ada_bias": scatter_about(key_of[3], (6 * D,), 0.3, 4.0, (), jnp.float32),
        "query_weight": scatter_about(key_of[4], (D, D), D ** -0.5, 0.1875, ((1, 4),)),
        "query_bias": scatter_about(key_of[5], (D,), 0.3, 4.0, ((0, 4),), jnp.float32),
        "key_weight": scatter_about(key_of[6], (D, D), D ** -0.5, 0.1875, ((1, 4),)),
        "value_weight": scatter_about(key_of[7], (D, D), D ** -0.5, 0.1875, ((1, 4),)),
        "value_bias": scatter_about(key_of[8], (D,), 0.3, 4.0, ((0, 4),), jnp.float32),
        "out_weight": scatter_about(key_of[9], (D, D), (D // 16) ** -0.5, 0.75, ((0, 4),)),
        "out_bias": scatter_about(key_of[10], (D,), 0.3, 4.0, (), jnp.float32),
        "up_weight": scatter_about(key_of[11], (D, FF), D ** -0.5, 0.1875, ((1, 4),)),
        "up_bias": scatter_about(key_of[12], (FF,), 0.3, 4.0, ((0, 4),), jnp.float32),
        "down_weight": scatter_about(key_of[13], (FF, D), FF ** -0.5, 0.09375, ((0, 4),)),
        "down_bias": scatter_about(key_of[14], (D,), 0.3, 4.0, (), jnp.float32),
        "clip_limit": draw_clip_limit(jax.random.fold_in(key_of[17], 71), 0),
        "cotangent": scatter_about(key_of[16], (TOKENS, D), 1.0, 6.0, ((0, 8),)),
    }


@jax.custom_vjp
def low(v):
    return lax.optimization_barrier(v.astype(jnp.bfloat16)).astype(jnp.float32)

@jax.custom_vjp
def low_back(v):
    return v

def low_keep(v):
    return (low(v), None)

def low_pass(kept, grad):
    return (grad,)

def back_keep(v):
    return (v, None)

def back_low(kept, grad):
    return (low(grad),)
low.defvjp(low_keep, low_pass)
low_back.defvjp(back_keep, back_low)
EPSILON = 1e-06
PRECISE = lax.Precision.HIGHEST

def layer_norm(row_values):
    centered = row_values - lax.optimization_barrier(jnp.mean(row_values, axis=-1, keepdims=True))
    return centered * lax.rsqrt(lax.optimization_barrier(jnp.mean(centered * centered, axis=-1, keepdims=True)) + EPSILON)

def project(activ, matrix):
    return jnp.einsum('lsd,de->lse', activ, matrix, precision=PRECISE)

def attend(block):
    query_all, key_all, value_all = block
    head_shape = (SEQ, H, HD)
    scores = low_back(jnp.einsum('qhd,khd->hqk', query_all.reshape(head_shape), key_all.reshape(head_shape), precision=PRECISE) * (1.0 / math.sqrt(HD)))
    probs = jax.nn.softmax(scores, axis=-1)
    mixed = jnp.einsum('hqk,khd->qhd', low(probs), value_all.reshape(head_shape), precision=PRECISE)
    return (mixed.reshape(SEQ, D), lax.optimization_barrier(jnp.max(scores, axis=(1, 2))))

def forward(tokens, condition, ada_weight, ada_bias, query_weight, query_bias, key_weight, value_weight, value_bias, out_weight, out_bias, up_weight, up_bias, down_weight, down_bias):
    modulation = low_back(jnp.dot(low(jax.nn.silu(condition)), ada_weight, precision=PRECISE) + ada_bias)
    pieces = [modulation[:, None, index * D:(index + 1) * D] for index in range(6)]
    stream = tokens.reshape(LATENTS, SEQ, D)
    hidden_a = low(layer_norm(stream) * (1.0 + pieces[1]) + pieces[0])
    queries = low(low_back(project(hidden_a, query_weight) + query_bias))
    keys = low(low_back(project(hidden_a, key_weight)))
    values = low(low_back(project(hidden_a, value_weight) + value_bias))
    mixed, peaks = lax.map(jax.checkpoint(attend), (queries, keys, values))
    heads_out = low(low_back(mixed))
    branch_a = low_back(project(heads_out, out_weight) + out_bias)
    middle = stream + pieces[2] * branch_a
    hidden_b = low(layer_norm(middle) * (1.0 + pieces[4]) + pieces[3])
    before = low_back(project(hidden_b, up_weight) + up_bias)
    act_b = low(jax.nn.gelu(before, approximate=True))
    branch_b = low_back(project(act_b, down_weight) + down_bias)
    result = middle + pieces[5] * branch_b
    return (result.reshape(LATENTS * SEQ, D), lax.optimization_barrier(jnp.max(peaks, axis=0)))

def reference(tokens, condition, ada_weight, ada_bias, query_weight, query_bias, key_weight, value_weight, value_bias, out_weight, out_bias, up_weight, up_bias, down_weight, down_bias, clip_limit, cotangent):
    result, pullback, head_max = jax.vjp(forward, tokens.astype(jnp.float32), condition, ada_weight.astype(jnp.float32), ada_bias, query_weight.astype(jnp.float32), query_bias, key_weight.astype(jnp.float32), value_weight.astype(jnp.float32), value_bias, out_weight.astype(jnp.float32), out_bias, up_weight.astype(jnp.float32), up_bias, down_weight.astype(jnp.float32), down_bias, has_aux=True)
    grads = pullback(cotangent.astype(jnp.float32))
    factor = jnp.sqrt(clip_limit / jnp.maximum(head_max, clip_limit))
    column_factor = jnp.repeat(factor, HD)
    return (result.astype(jnp.bfloat16), grads[0].astype(jnp.bfloat16), grads[1], grads[2], grads[3], grads[4], grads[5], grads[6], grads[7], grads[8], grads[9], grads[10], grads[11], grads[12], grads[13], grads[14], head_max, query_weight.astype(jnp.float32) * column_factor, query_bias * column_factor, key_weight.astype(jnp.float32) * column_factor)
```

```python
import math

import jax
import jax.numpy as jnp
from jax import lax
from jax.sharding import PartitionSpec as P

EPSILON = 1e-06
F32 = jnp.float32
BF16 = jnp.bfloat16


def layer_norm(row_values):
    centered = row_values - jnp.mean(row_values, axis=-1, keepdims=True)
    inv_std = lax.rsqrt(jnp.mean(centered * centered, axis=-1, keepdims=True) + EPSILON)
    return (centered * inv_std, inv_std)


def norm_back(grad_norm, normed, inv_std):
    return inv_std * (
        grad_norm
        - jnp.mean(grad_norm, axis=-1, keepdims=True)
        - normed * jnp.mean(grad_norm * normed, axis=-1, keepdims=True)
    )


def contract_rows(operand_a, operand_b):
    return lax.dot_general(
        operand_a, operand_b, (((0,), (0,)), ((), ())), preferred_element_type=F32
    )


def dot_transposed(operand_a, operand_b):
    return lax.dot_general(
        operand_a, operand_b, (((1,), (1,)), ((), ())), preferred_element_type=F32
    )


def gelu_tanh(inputs):
    return jax.nn.gelu(inputs, approximate=True)


def swap(value, axis, bit):
    size = lax.axis_size(axis)
    return lax.ppermute(value, axis, [(i, i ^ bit) for i in range(size)])


def own_order(rows):
    size = lax.axis_size("tensor")
    quarter = rows.shape[0] // size
    me = lax.axis_index("tensor")
    return jnp.concatenate(
        [lax.dynamic_slice_in_dim(rows, (me ^ j) * quarter, quarter, 0) for j in range(size)]
    )


def gather_quarters(share):
    far = swap(share, "tensor", 2)
    near = swap(share, "tensor", 1)
    return jnp.concatenate([share, near, far, swap(far, "tensor", 1)])


def reduce_quarters(rows):
    quarter = rows.shape[0] // 4
    block = [rows[j * quarter : (j + 1) * quarter] for j in range(4)]
    far = block[2].astype(F32) + swap(block[3], "tensor", 1).astype(F32)
    got = swap(far.astype(BF16), "tensor", 2)
    mine = block[0].astype(F32) + swap(block[1], "tensor", 1).astype(F32)
    return mine + got.astype(F32)


def total(value, axis, join=jnp.add):
    bit = 1
    while bit < lax.axis_size(axis):
        value = join(value, swap(value, axis, bit))
        bit *= 2
    return value


def gather_rows(row, axis):
    size = lax.axis_size(axis)
    held = row
    bit = 1
    while bit < size:
        held = jnp.concatenate([held, swap(held, axis, bit)])
        bit *= 2
    me = lax.axis_index(axis)
    bit = 1
    while bit < size:
        split = held.reshape(size // (2 * bit), 2, bit, -1)
        held = jnp.where((me & bit) != 0, jnp.flip(split, 1), split).reshape(size, -1)
        bit *= 2
    return held


def ring_order(size):
    return list(range(0, size, 2)) + list(range(size - 1, 0, -2))


def ring_place(size):
    order = ring_order(size)
    place = [0] * size
    for at, device in enumerate(order):
        place[device] = at
    return jnp.take(jnp.array(place, jnp.int32), lax.axis_index("dp"))


def ring_send(value, way):
    order = ring_order(lax.axis_size("dp"))
    size = len(order)
    return lax.ppermute(
        value, "dp", [(order[i], order[(i + way) % size]) for i in range(size)]
    )


def ring_sum(partial):
    rows, width = partial.shape
    size = lax.axis_size("dp")
    if size != 8:
        part = lax.psum_scatter(
            partial.astype(F32), "dp", scatter_dimension=0, tiled=True
        ).astype(BF16)
        return lax.all_gather(part, "dp", axis=0, tiled=True).astype(F32)
    half = rows // size // 2
    place = ring_place(size)
    pieces = partial.astype(BF16).reshape(size, 2, half, width)

    def local(chunk, side):
        return lax.dynamic_slice(
            pieces, (lax.rem(chunk + 2 * size, size), side, 0, 0), (1, 1, half, width)
        )

    moving = [local(place - 1, 0), local(place + 1, 1)]
    for step in range(size - 1):
        for side, way in ((0, 1), (1, -1)):
            got = ring_send(moving[side], way).astype(F32)
            moving[side] = (got + local(place - way * (2 + step), side).astype(F32)).astype(BF16)
    out = jnp.zeros((size, 2, half, width), F32)
    for side in (0, 1):
        out = lax.dynamic_update_slice(out, moving[side].astype(F32), (place, side, 0, 0))
    for step in range(size - 1):
        for side, way in ((0, 1), (1, -1)):
            moving[side] = ring_send(moving[side], way)
            chunk = lax.rem(place - way * (1 + step) + 2 * size, size)
            out = lax.dynamic_update_slice(out, moving[side].astype(F32), (chunk, side, 0, 0))
    return out.reshape(rows, width)


def sum_dp(value):
    if lax.axis_size("dp") == 8:
        return total(value, "dp")
    return lax.psum(value, "dp")


def split_vector(vector, lengths):
    pieces = []
    offset = 0
    for length in lengths:
        pieces.append(vector[offset : offset + length])
        offset = offset + length
    return pieces


def shards(
    tokens,
    condition,
    ada_weight,
    ada_bias,
    query_weight,
    query_bias,
    key_weight,
    value_weight,
    value_bias,
    out_weight,
    out_bias,
    up_weight,
    up_bias,
    down_weight,
    down_bias,
    clip_limit,
    cotangent,
):
    model_width = tokens.shape[1]
    token_rows = tokens.shape[0]
    assert condition.shape[0] == 1 and lax.axis_size("tensor") == 4
    share_rows = token_rows // 4
    local_heads = clip_limit.shape[0]
    head_width = query_weight.shape[1]
    head_size = head_width // local_heads
    score_scale = 1.0 / math.sqrt(head_size)

    cond_act, silu_back = jax.vjp(jax.nn.silu, condition)
    cond_low = cond_act.astype(BF16)
    modulation = (
        total(jnp.dot(cond_low, ada_weight, preferred_element_type=F32), "tensor") + ada_bias
    )
    shift_a, scale_a, gate_a, shift_b, scale_b, gate_b = [
        modulation[:, i * model_width : (i + 1) * model_width] for i in range(6)
    ]
    rows_a = own_order(tokens)
    grad_rows = own_order(cotangent)
    residual = rows_a.astype(F32)
    normed_one, inv_one = layer_norm(residual)
    hidden_one = (normed_one * (1.0 + scale_a) + shift_a).astype(BF16)
    queries = (jnp.dot(hidden_one, query_weight, preferred_element_type=F32) + query_bias).astype(
        BF16
    )
    keys = jnp.dot(hidden_one, key_weight, preferred_element_type=F32).astype(BF16)
    values = (jnp.dot(hidden_one, value_weight, preferred_element_type=F32) + value_bias).astype(
        BF16
    )
    head_shape = (token_rows, local_heads, head_size)
    query_heads = queries.reshape(head_shape)
    key_heads = keys.reshape(head_shape)
    value_heads = values.reshape(head_shape)
    scores = (
        jnp.einsum("qhd,khd->hqk", query_heads, key_heads, preferred_element_type=F32)
        * score_scale
    )
    peak = jnp.max(scores, axis=2, keepdims=True)
    log_total = peak + jnp.log(jnp.sum(jnp.exp(scores - peak), axis=2, keepdims=True))
    weights = jnp.exp(scores - log_total).astype(BF16)
    heads_out = jnp.einsum(
        "hqk,khd->qhd", weights, value_heads, preferred_element_type=F32
    ).astype(BF16)
    attn_flat = heads_out.reshape(token_rows, -1)
    head_peak = jnp.max(peak[:, :, 0], axis=1)
    if lax.axis_size("dp") == 8:
        head_peak = total(head_peak, "dp", jnp.maximum)
    else:
        head_peak = lax.pmax(head_peak, "dp")
    factor = jnp.sqrt(clip_limit / jnp.maximum(head_peak, clip_limit))
    column_factor = jnp.repeat(factor, head_size)
    clipped_query = query_weight.astype(F32) * column_factor
    clipped_bias = query_bias * column_factor
    clipped_key = key_weight.astype(F32) * column_factor

    branch = jnp.dot(attn_flat, out_weight, preferred_element_type=F32).astype(BF16)
    attn_share = reduce_quarters(branch) + out_bias
    middle = residual[:share_rows] + gate_a * attn_share
    normed_two, inv_two = layer_norm(middle)
    hidden_share = (normed_two * (1.0 + scale_b) + shift_b).astype(BF16)
    hidden_two = gather_quarters(hidden_share)
    before = jnp.dot(hidden_two, up_weight, preferred_element_type=F32) + up_bias
    activation, gelu_back = jax.vjp(gelu_tanh, before)
    act_low = activation.astype(BF16)
    grad_feed = (grad_rows.astype(F32) * gate_b).astype(BF16)
    grad_before = gelu_back(dot_transposed(grad_feed, down_weight))[0].astype(BF16)
    grad_two = reduce_quarters(dot_transposed(grad_before, up_weight).astype(BF16))
    mlp_share = (
        reduce_quarters(jnp.dot(act_low, down_weight, preferred_element_type=F32).astype(BF16))
        + down_bias
    )
    block_out = (middle + gate_b * mlp_share).astype(BF16)
    grad_down_w = ring_sum(contract_rows(act_low, grad_feed))
    grad_down_b = jnp.sum(grad_feed.astype(F32), axis=0)
    grad_up_w = ring_sum(contract_rows(hidden_two, grad_before))
    grad_up_b = jnp.sum(grad_before.astype(F32), axis=0)

    grad_out_share = grad_rows[:share_rows].astype(F32)
    grad_middle = grad_out_share + norm_back(grad_two * (1.0 + scale_b), normed_two, inv_two)
    grad_branch = gather_quarters((grad_middle * gate_a).astype(BF16))
    grad_out_w = ring_sum(contract_rows(grad_branch, attn_flat)).T
    grad_out_b = jnp.sum(grad_branch.astype(F32), axis=0)
    grad_heads = dot_transposed(grad_branch, out_weight).astype(BF16).reshape(head_shape)

    probs = jnp.exp(scores - log_total)
    grad_value = jnp.einsum(
        "hqk,qhd->khd", probs.astype(BF16), grad_heads, preferred_element_type=F32
    )
    grad_probs = jnp.einsum("qhd,khd->hqk", grad_heads, value_heads, preferred_element_type=F32)
    grad_scores = (
        probs * (grad_probs - jnp.sum(probs * grad_probs, axis=2, keepdims=True))
    ).astype(BF16)
    grad_query = (
        jnp.einsum("hqk,khd->qhd", grad_scores, key_heads, preferred_element_type=F32)
        * score_scale
    )
    grad_key = (
        jnp.einsum("hqk,qhd->khd", grad_scores, query_heads, preferred_element_type=F32)
        * score_scale
    )
    flat = (token_rows, head_width)
    grad_query_rows = grad_query.astype(BF16).reshape(flat)
    grad_key_rows = grad_key.astype(BF16).reshape(flat)
    grad_value_rows = grad_value.astype(BF16).reshape(flat)
    grad_qkv = jnp.concatenate([grad_query_rows, grad_key_rows, grad_value_rows], axis=1)
    weight_qkv = jnp.concatenate([query_weight, key_weight, value_weight], axis=1)
    grad_one = reduce_quarters(dot_transposed(grad_qkv, weight_qkv).astype(BF16))
    grad_qkv_w = ring_sum(contract_rows(hidden_one, grad_qkv))
    grad_query_w = grad_qkv_w[:, :head_width]
    grad_key_w = grad_qkv_w[:, head_width : 2 * head_width]
    grad_value_w = grad_qkv_w[:, 2 * head_width :]
    grad_query_b = jnp.sum(grad_query_rows.astype(F32), axis=0)
    grad_value_b = jnp.sum(grad_value_rows.astype(F32), axis=0)
    normed_share = normed_one[:share_rows]
    inv_share = inv_one[:share_rows]
    grad_tokens = (
        grad_middle + norm_back(grad_one * (1.0 + scale_a), normed_share, inv_share)
    ).astype(BF16)

    def column_sum(rows):
        return jnp.sum(rows, axis=0, keepdims=True)

    mod_terms = jnp.concatenate(
        [
            column_sum(grad_one),
            column_sum(grad_one * normed_share),
            column_sum(grad_middle * attn_share),
            column_sum(grad_two),
            column_sum(grad_two * normed_two),
            column_sum(grad_out_share * mlp_share),
        ],
        axis=1,
    )
    grad_mod = total(mod_terms, "tensor").astype(BF16)
    grad_condition = silu_back(dot_transposed(grad_mod, ada_weight))[0]
    factors = jnp.concatenate([cond_low, grad_mod], axis=1)
    if lax.axis_size("dp") == 8:
        factors = gather_rows(factors, "dp")
    else:
        factors = lax.all_gather(factors, "dp", axis=0, tiled=True)
    cond_width = cond_low.shape[1]
    grad_ada_w = contract_rows(factors[:, :cond_width], factors[:, cond_width:])
    grad_ada_b = jnp.sum(factors[:, cond_width:].astype(F32), axis=0)
    bias_terms = [grad_query_b, grad_value_b, grad_up_b, grad_out_b, grad_down_b]
    full_bias = sum_dp(jnp.concatenate(bias_terms))
    full_qb, full_vb, full_ub, full_ob, full_db = split_vector(
        full_bias, [term.shape[0] for term in bias_terms]
    )
    return (
        block_out,
        grad_tokens,
        grad_condition,
        grad_ada_w,
        grad_ada_b,
        grad_query_w,
        full_qb,
        grad_key_w,
        grad_value_w,
        full_vb,
        grad_out_w,
        full_ob,
        grad_up_w,
        full_ub,
        grad_down_w,
        full_db,
        head_peak,
        clipped_query,
        clipped_bias,
        clipped_key,
    )


def solution(mesh):
    return jax.shard_map(
        shards,
        mesh=mesh,
        in_specs=(
            P("dp", None),
            P("dp", "tensor"),
            P("tensor", None),
            P(),
            P(None, "tensor"),
            P("tensor"),
            P(None, "tensor"),
            P(None, "tensor"),
            P("tensor"),
            P("tensor", None),
            P(),
            P(None, "tensor"),
            P("tensor"),
            P("tensor", None),
            P(),
            P("tensor"),
            P("dp", None),
        ),
        out_specs=(
            P(("dp", "tensor"), None),
            P(("dp", "tensor"), None),
            P("dp", "tensor"),
            P("tensor", None),
            P(),
            P(None, "tensor"),
            P("tensor"),
            P(None, "tensor"),
            P(None, "tensor"),
            P("tensor"),
            P("tensor", None),
            P(),
            P(None, "tensor"),
            P("tensor"),
            P("tensor", None),
            P(),
            P("tensor"),
            P(None, "tensor"),
            P("tensor"),
            P(None, "tensor"),
        ),
        check_vma=False,
    )
```

```python
import math

import jax
import jax.numpy as jnp
from jax import lax
from jax.experimental import pallas as pl
from jax.experimental.pallas import tpu as pltpu
from jax.sharding import PartitionSpec as P

EPSILON = 1e-06
F32 = jnp.float32
BF16 = jnp.bfloat16


def layer_norm(row_values):
    centered = row_values - jnp.mean(row_values, axis=-1, keepdims=True)
    inv_std = lax.rsqrt(jnp.mean(centered * centered, axis=-1, keepdims=True) + EPSILON)
    return (centered * inv_std, inv_std)


def norm_back(grad_norm, normed, inv_std):
    return inv_std * (
        grad_norm
        - jnp.mean(grad_norm, axis=-1, keepdims=True)
        - normed * jnp.mean(grad_norm * normed, axis=-1, keepdims=True)
    )


def contract_rows(operand_a, operand_b):
    return lax.dot_general(
        operand_a, operand_b, (((0,), (0,)), ((), ())), preferred_element_type=F32
    )


def dot_transposed(operand_a, operand_b):
    return lax.dot_general(
        operand_a, operand_b, (((1,), (1,)), ((), ())), preferred_element_type=F32
    )


def gelu_tanh(inputs):
    return jax.nn.gelu(inputs, approximate=True)


def swap(value, axis, bit):
    size = lax.axis_size(axis)
    return lax.ppermute(value, axis, [(i, i ^ bit) for i in range(size)])


def own_order(rows):
    size = lax.axis_size("tensor")
    quarter = rows.shape[0] // size
    me = lax.axis_index("tensor")
    return jnp.concatenate(
        [lax.dynamic_slice_in_dim(rows, (me ^ j) * quarter, quarter, 0) for j in range(size)]
    )


def gather_quarters(share):
    far = swap(share, "tensor", 2)
    near = swap(share, "tensor", 1)
    return jnp.concatenate([share, near, far, swap(far, "tensor", 1)])


def reduce_quarters(rows):
    quarter = rows.shape[0] // 4
    block = [rows[j * quarter : (j + 1) * quarter] for j in range(4)]
    far = block[2].astype(F32) + swap(block[3], "tensor", 1).astype(F32)
    got = swap(far.astype(BF16), "tensor", 2)
    mine = block[0].astype(F32) + swap(block[1], "tensor", 1).astype(F32)
    return mine + got.astype(F32)


def total(value, axis, join=jnp.add):
    bit = 1
    while bit < lax.axis_size(axis):
        value = join(value, swap(value, axis, bit))
        bit *= 2
    return value


def gather_rows(row, axis):
    size = lax.axis_size(axis)
    held = row
    bit = 1
    while bit < size:
        held = jnp.concatenate([held, swap(held, axis, bit)])
        bit *= 2
    me = lax.axis_index(axis)
    bit = 1
    while bit < size:
        split = held.reshape(size // (2 * bit), 2, bit, -1)
        held = jnp.where((me & bit) != 0, jnp.flip(split, 1), split).reshape(size, -1)
        bit *= 2
    return held


def by_distance(blocks, size):
    me = lax.axis_index("dp")
    rows = blocks.shape[0] // size
    return jnp.concatenate(
        [lax.dynamic_slice_in_dim(blocks, (me ^ k) * rows, rows, 0) for k in range(size)]
    )


def spread_sum(partial, bits):
    size = lax.axis_size("dp")
    if size != 8:
        part = lax.psum_scatter(partial.astype(F32), "dp", scatter_dimension=0, tiled=True)
        return lax.all_gather(part.astype(BF16), "dp", axis=0, tiled=True)
    rows = partial.shape[0] // size
    block = by_distance(partial, size)
    held = {k: block[k * rows : (k + 1) * rows] for k in range(size)}
    for bit in bits:
        keep = [k for k in held if not k & bit]
        got = swap(jnp.concatenate([held[k | bit] for k in keep]), "dp", bit)
        held = {
            k: (held[k].astype(F32) + got[i * rows : (i + 1) * rows].astype(F32)).astype(BF16)
            for i, k in enumerate(keep)
        }
    for bit in bits[::-1]:
        keep = sorted(held)
        got = swap(jnp.concatenate([held[k] for k in keep]), "dp", bit)
        for i, k in enumerate(keep):
            held[k | bit] = got[i * rows : (i + 1) * rows]
    return by_distance(jnp.concatenate([held[k] for k in range(size)]), size)


def scatter_sum(partial):
    part = lax.psum_scatter(partial, "dp", scatter_dimension=0, tiled=True)
    return lax.all_gather(part, "dp", axis=0, tiled=True)


LANES = 128


def head_pads(heads, size):
    row = lax.broadcasted_iota(jnp.int32, (heads * size, heads * LANES), 0)
    col = lax.broadcasted_iota(jnp.int32, (heads * size, heads * LANES), 1)
    head = col // LANES
    lane = col - head * LANES
    return ((row == head * size + lane) & (lane < size)).astype(F32).astype(BF16)


def dot(a, b, dims=((1,), (0,))):
    return lax.dot_general(a, b, (dims, ((), ())), preferred_element_type=F32)


def attend_kernel(
    heads, size, hidden, qw, qb, kw, vw, vb, ow, q_out, k_out, v_out, probs_out, peak_out,
    heads_out, branch_out, k_pad, v_pad,
):
    step = pl.program_id(0)
    rows = q_out.shape[0]
    pads = head_pads(heads, size)

    @pl.when(step == 0)
    def _():
        keys = dot(hidden[...], kw[...]).astype(BF16)
        values = (dot(hidden[...], vw[...]) + vb[...]).astype(BF16)
        k_out[...] = keys
        v_out[...] = values
        k_pad[...] = dot(keys, pads).astype(BF16)
        v_pad[...] = dot(values, pads).astype(BF16)

    part = hidden[pl.ds(pl.multiple_of(step * rows, rows), rows), :]
    queries = (dot(part, qw[...]) + qb[...]).astype(BF16)
    q_out[...] = queries
    q_pad = dot(queries, pads).astype(BF16)
    mixed = []
    for h in range(heads):
        cols = slice(h * LANES, (h + 1) * LANES)
        scores = dot(k_pad[:, cols], q_pad[:, cols], ((1,), (1,))) * (1.0 / math.sqrt(size))
        peak = jnp.max(scores, axis=0, keepdims=True)
        peak_out[h : h + 1, :] = peak
        weights = jnp.exp(scores - peak)
        weights = weights * (1.0 / jnp.sum(weights, axis=0, keepdims=True))
        probs = weights.astype(BF16)
        probs_out[h] = probs
        mixed.append(dot(v_pad[:, cols], probs, ((0,), (0,))).T.astype(BF16))
    flat = dot(jnp.concatenate(mixed, axis=1), pads, ((1,), (1,))).astype(BF16)
    heads_out[...] = flat
    branch_out[...] = dot(flat, ow[...]).astype(BF16)


def attend(heads, hidden, qw, qb, kw, vw, vb, ow):
    rows, width = hidden.shape
    head_width = qw.shape[1]
    steps = 4
    part = rows // steps
    full = lambda shape: pl.BlockSpec(shape, lambda i: (0, 0), pipeline_mode=pl.Buffered(1))
    split = lambda n: pl.BlockSpec((part, n), lambda i: (i, 0))
    low = lambda *shape: jax.ShapeDtypeStruct(shape, BF16)
    return pl.pallas_call(
        lambda *refs: attend_kernel(heads, head_width // heads, *refs),
        grid=(steps,),
        in_specs=[
            full((rows, width)), full(qw.shape), full((1, head_width)), full(kw.shape),
            full(vw.shape), full((1, head_width)), full(ow.shape),
        ],
        out_specs=[
            split(head_width), full((rows, head_width)), full((rows, head_width)),
            pl.BlockSpec((heads, rows, part), lambda i: (0, 0, i)),
            pl.BlockSpec((heads, part), lambda i: (0, i)),
            split(head_width), split(width),
        ],
        out_shape=[
            low(rows, head_width), low(rows, head_width), low(rows, head_width),
            low(heads, rows, rows), jax.ShapeDtypeStruct((heads, rows), F32),
            low(rows, head_width), low(rows, width),
        ],
        scratch_shapes=[pltpu.VMEM((rows, heads * LANES), BF16)] * 2,
        compiler_params=pltpu.CompilerParams(vmem_limit_bytes=48 << 20),
        name="attend",
    )(hidden, qw, qb[None], kw, vw, vb[None], ow)


def attend_back_kernel(
    heads, size, grad, ow, q, k, v, probs_in, dq_out, dk_out, dv_out, k_pad, v_pad, dk, dv
):
    step = pl.program_id(0)
    pads = head_pads(heads, size)
    scale = 1.0 / math.sqrt(size)

    @pl.when(step == 0)
    def _():
        k_pad[...] = dot(k[...], pads).astype(BF16)
        v_pad[...] = dot(v[...], pads).astype(BF16)
        dk[...] = jnp.zeros_like(dk)
        dv[...] = jnp.zeros_like(dv)

    grad_heads = dot(grad[...], ow[...], ((1,), (1,))).astype(BF16)
    g_pad = dot(grad_heads, pads).astype(BF16)
    q_pad = dot(q[...], pads).astype(BF16)
    queries = []
    for h in range(heads):
        cols = slice(h * LANES, (h + 1) * LANES)
        low = probs_in[h]
        probs = low.astype(F32)
        grad_probs = dot(v_pad[:, cols], g_pad[:, cols], ((1,), (1,)))
        mean = jnp.sum(probs * grad_probs, axis=0, keepdims=True)
        grad_scores = (probs * (grad_probs - mean)).astype(BF16)
        dv[:, cols] += dot(low, g_pad[:, cols])
        dk[:, cols] += dot(grad_scores, q_pad[:, cols])
        queries.append(
            (dot(k_pad[:, cols], grad_scores, ((0,), (0,))) * scale).T.astype(BF16)
        )
    dq_out[...] = dot(jnp.concatenate(queries, axis=1), pads, ((1,), (1,))).astype(BF16)

    @pl.when(step == pl.num_programs(0) - 1)
    def _():
        dk_out[...] = dot((dk[...] * scale).astype(BF16), pads, ((1,), (1,))).astype(BF16)
        dv_out[...] = dot(dv[...].astype(BF16), pads, ((1,), (1,))).astype(BF16)


def attend_back(heads, grad, ow, q, k, v, probs):
    rows, width = grad.shape
    head_width = q.shape[1]
    steps = 4
    part = rows // steps
    full = lambda shape: pl.BlockSpec(shape, lambda i: (0, 0), pipeline_mode=pl.Buffered(1))
    split = lambda n: pl.BlockSpec((part, n), lambda i: (i, 0))
    padded = (rows, heads * LANES)
    return pl.pallas_call(
        lambda *refs: attend_back_kernel(heads, head_width // heads, *refs),
        grid=(steps,),
        in_specs=[
            split(width), full(ow.shape), split(head_width), full(k.shape), full(v.shape),
            pl.BlockSpec((heads, rows, part), lambda i: (0, 0, i)),
        ],
        out_specs=[split(head_width), full(k.shape), full(v.shape)],
        out_shape=[jax.ShapeDtypeStruct((rows, head_width), BF16)] * 3,
        scratch_shapes=[pltpu.VMEM(padded, BF16)] * 2 + [pltpu.VMEM(padded, F32)] * 2,
        compiler_params=pltpu.CompilerParams(vmem_limit_bytes=48 << 20),
        name="attend_back",
    )(grad, ow, q, k, v, probs)


def sum_dp(value):
    if lax.axis_size("dp") == 8:
        return total(value, "dp")
    return lax.psum(value, "dp")


def split_vector(vector, lengths):
    pieces = []
    offset = 0
    for length in lengths:
        pieces.append(vector[offset : offset + length])
        offset = offset + length
    return pieces


def shards(
    tokens,
    condition,
    ada_weight,
    ada_bias,
    query_weight,
    query_bias,
    key_weight,
    value_weight,
    value_bias,
    out_weight,
    out_bias,
    up_weight,
    up_bias,
    down_weight,
    down_bias,
    clip_limit,
    cotangent,
):
    model_width = tokens.shape[1]
    token_rows = tokens.shape[0]
    assert condition.shape[0] == 1 and lax.axis_size("tensor") == 4
    share_rows = token_rows // 4
    local_heads = clip_limit.shape[0]
    head_width = query_weight.shape[1]
    head_size = head_width // local_heads

    cond_act, silu_back = jax.vjp(jax.nn.silu, condition)
    cond_low = cond_act.astype(BF16)
    modulation = (
        total(jnp.dot(cond_low, ada_weight, preferred_element_type=F32), "tensor") + ada_bias
    )
    shift_a, scale_a, gate_a, shift_b, scale_b, gate_b = [
        modulation[:, i * model_width : (i + 1) * model_width] for i in range(6)
    ]
    rows_a = own_order(tokens)
    grad_rows = own_order(cotangent)
    residual = rows_a.astype(F32)
    normed_one, inv_one = layer_norm(residual)
    hidden_one = (normed_one * (1.0 + scale_a) + shift_a).astype(BF16)
    queries, keys, values, probs, peaks, attn_flat, branch = attend(
        local_heads,
        hidden_one,
        query_weight,
        query_bias,
        key_weight,
        value_weight,
        value_bias,
        out_weight,
    )
    head_peak = jnp.max(peaks, axis=1)
    if lax.axis_size("dp") == 8:
        head_peak = total(head_peak, "dp", jnp.maximum)
    else:
        head_peak = lax.pmax(head_peak, "dp")
    factor = jnp.sqrt(clip_limit / jnp.maximum(head_peak, clip_limit))
    column_factor = jnp.repeat(factor, head_size)
    clipped_query = query_weight.astype(F32) * column_factor
    clipped_bias = query_bias * column_factor
    clipped_key = key_weight.astype(F32) * column_factor

    attn_share = reduce_quarters(branch) + out_bias
    middle = residual[:share_rows] + gate_a * attn_share
    normed_two, inv_two = layer_norm(middle)
    hidden_share = (normed_two * (1.0 + scale_b) + shift_b).astype(BF16)
    hidden_two = gather_quarters(hidden_share)
    before = jnp.dot(hidden_two, up_weight, preferred_element_type=F32) + up_bias
    activation, gelu_back = jax.vjp(gelu_tanh, before)
    act_low = activation.astype(BF16)
    grad_feed = (grad_rows.astype(F32) * gate_b).astype(BF16)
    grad_before = gelu_back(dot_transposed(grad_feed, down_weight))[0].astype(BF16)
    grad_two = reduce_quarters(dot_transposed(grad_before, up_weight).astype(BF16))
    mlp_share = (
        reduce_quarters(jnp.dot(act_low, down_weight, preferred_element_type=F32).astype(BF16))
        + down_bias
    )
    block_out = (middle + gate_b * mlp_share).astype(BF16)
    feed_w = scatter_sum(
        jnp.concatenate(
            [
                contract_rows(act_low, grad_feed).astype(BF16),
                contract_rows(hidden_two, grad_before).astype(BF16),
            ]
        )
    ).astype(F32)
    grad_down_w = feed_w[: act_low.shape[1]]
    grad_up_w = feed_w[act_low.shape[1] :]
    grad_down_b = jnp.sum(grad_feed.astype(F32), axis=0)
    grad_up_b = jnp.sum(grad_before.astype(F32), axis=0)

    grad_out_share = grad_rows[:share_rows].astype(F32)
    grad_middle = grad_out_share + norm_back(grad_two * (1.0 + scale_b), normed_two, inv_two)
    grad_branch = gather_quarters((grad_middle * gate_a).astype(BF16))
    grad_out_b = jnp.sum(grad_branch.astype(F32), axis=0)
    grad_query_rows, grad_key_rows, grad_value_rows = attend_back(
        local_heads, grad_branch, out_weight, queries, keys, values, probs
    )
    grad_qkv = jnp.concatenate([grad_query_rows, grad_key_rows, grad_value_rows], axis=1)
    weight_qkv = jnp.concatenate([query_weight, key_weight, value_weight], axis=1)
    grad_one = reduce_quarters(dot_transposed(grad_qkv, weight_qkv).astype(BF16))
    first_w = spread_sum(
        contract_rows(
            hidden_one, jnp.concatenate([grad_query_rows, grad_key_rows], axis=1)
        ).astype(BF16),
        (1, 2, 4),
    ).astype(F32)
    second_w = spread_sum(
        jnp.concatenate(
            [contract_rows(hidden_one, grad_value_rows), contract_rows(grad_branch, attn_flat)],
            axis=1,
        ).astype(BF16),
        (2, 4, 1),
    ).astype(F32)
    grad_query_w = first_w[:, :head_width]
    grad_key_w = first_w[:, head_width:]
    grad_value_w = second_w[:, :head_width]
    grad_out_w = second_w[:, head_width:].T
    grad_query_b = jnp.sum(grad_query_rows.astype(F32), axis=0)
    grad_value_b = jnp.sum(grad_value_rows.astype(F32), axis=0)
    normed_share = normed_one[:share_rows]
    inv_share = inv_one[:share_rows]
    grad_tokens = (
        grad_middle + norm_back(grad_one * (1.0 + scale_a), normed_share, inv_share)
    ).astype(BF16)

    def column_sum(rows):
        return jnp.sum(rows, axis=0, keepdims=True)

    mod_terms = jnp.concatenate(
        [
            column_sum(grad_one),
            column_sum(grad_one * normed_share),
            column_sum(grad_middle * attn_share),
            column_sum(grad_two),
            column_sum(grad_two * normed_two),
            column_sum(grad_out_share * mlp_share),
        ],
        axis=1,
    )
    grad_mod = total(mod_terms, "tensor").astype(BF16)
    grad_condition = silu_back(dot_transposed(grad_mod, ada_weight))[0]
    factors = jnp.concatenate([cond_low, grad_mod], axis=1)
    if lax.axis_size("dp") == 8:
        factors = gather_rows(factors, "dp")
    else:
        factors = lax.all_gather(factors, "dp", axis=0, tiled=True)
    cond_width = cond_low.shape[1]
    grad_ada_w = contract_rows(factors[:, :cond_width], factors[:, cond_width:])
    grad_ada_b = jnp.sum(factors[:, cond_width:].astype(F32), axis=0)
    bias_terms = [grad_query_b, grad_value_b, grad_up_b, grad_out_b, grad_down_b]
    full_bias = sum_dp(jnp.concatenate(bias_terms))
    full_qb, full_vb, full_ub, full_ob, full_db = split_vector(
        full_bias, [term.shape[0] for term in bias_terms]
    )
    return (
        block_out,
        grad_tokens,
        grad_condition,
        grad_ada_w,
        grad_ada_b,
        grad_query_w,
        full_qb,
        grad_key_w,
        grad_value_w,
        full_vb,
        grad_out_w,
        full_ob,
        grad_up_w,
        full_ub,
        grad_down_w,
        full_db,
        head_peak,
        clipped_query,
        clipped_bias,
        clipped_key,
    )


def solution(mesh):
    return jax.shard_map(
        shards,
        mesh=mesh,
        in_specs=(
            P("dp", None),
            P("dp", "tensor"),
            P("tensor", None),
            P(),
            P(None, "tensor"),
            P("tensor"),
            P(None, "tensor"),
            P(None, "tensor"),
            P("tensor"),
            P("tensor", None),
            P(),
            P(None, "tensor"),
            P("tensor"),
            P("tensor", None),
            P(),
            P("tensor"),
            P("dp", None),
        ),
        out_specs=(
            P(("dp", "tensor"), None),
            P(("dp", "tensor"), None),
            P("dp", "tensor"),
            P("tensor", None),
            P(),
            P(None, "tensor"),
            P("tensor"),
            P(None, "tensor"),
            P(None, "tensor"),
            P("tensor"),
            P("tensor", None),
            P(),
            P(None, "tensor"),
            P("tensor"),
            P("tensor", None),
            P(),
            P("tensor"),
            P(None, "tensor"),
            P("tensor"),
            P(None, "tensor"),
        ),
        check_vma=False,
    )
```
